32 devices in a mesh: grp: 4 (over z), dev: 8 (over y, x, core).
Axes of the slice: x: 2, y: 2, z: 4, core: 2. Of those that a mesh axis runs over, the one named last changes fastest.
Arguments:
- stamps: int32 [65536], P(('grp', 'dev')), may hold values from 0 to 14399, as said below
- account: int32 [65536], P(('grp', 'dev')), may hold values from 0 to 15, as said below
- kind: int32 [65536], P(('grp', 'dev')), may hold values from 0 to 5
- weight: bfloat16 [65536], P(('grp', 'dev')), may hold values from -3 to 3
- used: int32 [32, 64], P(('grp', 'dev')), may hold values from 1 to 32, as said below
Outputs:
- pair_profile: float32 [36, 1024], P(None, 'dev')
- triple_profile: float32 [8, 1024], P(None, 'dev')
The draws below stay inside these ranges and needn't reach their ends.
Inputs may be any that keep to these rules, and one draw needn't show every extreme that they name: `account`: small values are more common. `stamps`: an event of sender r lies in time range r // 8: its stamp is at least (r // 8) * 3600 and below that plus 3600. `used`: column 0 of every row equals 32.
All inputs are finite; a program needn't handle non-finite values.
Results may differ from the reference program's by a relative error of at most 0.0003.
Values sent between devices are 32-bit elements; how exact they have to be, the bound alone decides.
A program may use at most 64 MiB of HBM per device.

```python
import jax
import jax.numpy as jnp
from jax import lax

DELTA = 3600
BLK = 256
ACC_BLK = 16
NB = 8
CAP = 32
ACCOUNTS = 1024
EVENTS = 65536
N_GRP = 4
N_DEV = 8


def draw_stamps(key, part):
    index = jnp.arange(EVENTS, dtype=jnp.int32)
    group = index // (N_DEV * NB * BLK)
    offset = jax.random.randint(key, (EVENTS,), 0, DELTA, dtype=jnp.int32)
    return offset + group * DELTA


def draw_account(key, part):
    first = jax.random.randint(jax.random.fold_in(key, 1), (EVENTS,), 0, ACC_BLK, dtype=jnp.int32)
    second = jax.random.randint(jax.random.fold_in(key, 2), (EVENTS,), 0, ACC_BLK, dtype=jnp.int32)
    return jnp.minimum(first, second)


def draw_used(key, part):
    counts = jax.random.randint(key, (N_GRP * N_DEV, N_DEV * NB), 1, CAP + 1, dtype=jnp.int32)
    return counts.at[:, 0].set(CAP)


def with_ends(drawn, stream_key, smallest, top_value):
    longest = drawn.shape.index(max(drawn.shape))
    spots = []
    for shift in (0, 1):
        where = [jax.random.randint(jax.random.fold_in(stream_key, axis), (), 0, length) for axis, length in enumerate(drawn.shape)]
        where[longest] = (where[longest] + shift) % drawn.shape[longest]
        spots.append(tuple(where))
    return drawn.at[spots[0]].set(smallest).at[spots[1]].set(top_value)


def level_of(rng, extent, cuts, smallest, largest):
    def one(position, shards_of):
        steps = jax.random.uniform(jax.random.fold_in(jax.random.fold_in(rng, 6), position), (shards_of,), jnp.float32, smallest / len(cuts), largest / len(cuts))
        return jnp.repeat(jnp.exp(steps), extent[position] // shards_of).reshape((-1,) + (1,) * (len(extent) - position - 1))

    loudness = one(*cuts[0])
    for cut in cuts[1:]:
        loudness = loudness * one(*cut)
    return loudness


def bell_draw(key, extent, scale, most, split=(), held_as=jnp.bfloat16):
    gain = level_of(key, extent, split, -0.22, 0.18) if split else 1.0
    values = jax.random.normal(key, extent, jnp.float32) * scale * gain
    return jnp.minimum(jnp.maximum(values, -most), most).astype(held_as)


def setup_inputs(seed: int = 0) -> dict:
    keys = jax.random.split(jax.random.key(seed), 6)
    return {
        "stamps": draw_stamps(jax.random.fold_in(keys[5], 71), 0),
        "account": draw_account(jax.random.fold_in(keys[5], 71), 0),
        "kind": with_ends(jax.random.randint(keys[2], (EVENTS,), 0, 6), jax.random.fold_in(keys[2], 1), 0, 5).astype(jnp.int32),
        "weight": bell_draw(keys[3], (EVENTS,), 0.5, 3.0, ((0, 32),)),
        "used": draw_used(jax.random.fold_in(keys[5], 71), 0),
    }


def count_block(own_rows, prior_rows):
    fields = jnp.concatenate([prior_rows, own_rows], axis=1)
    stamp, local, kinds, wt = fields[0], fields[1], fields[2], fields[3]
    blk = own_rows.shape[1]
    gap = stamp[None, :] - stamp[:, None]
    linked = (local[:, None] == local[None, :]) & (gap > 0.0) & (gap <= DELTA)
    link_all = linked.astype(jnp.float32)
    link_own = link_all[:, blk:]
    classes = (kinds[:, None] == jnp.arange(6).astype(jnp.float32)[None, :]).astype(jnp.float32) * wt[:, None]
    earlier = jnp.dot(link_own.T, classes, precision=lax.Precision.HIGHEST)
    later = classes[blk:]
    pair_terms = (earlier[:, :, None] * later[:, None, :]).reshape(blk, 36)
    owners_hot = (local[blk:, None] == jnp.arange(ACC_BLK).astype(jnp.float32)[None, :]).astype(jnp.float32)
    pairs = jnp.dot(pair_terms.T, owners_hot, precision=lax.Precision.HIGHEST)
    dirs = jnp.stack([wt * (kinds < 2.5), wt * (kinds > 2.5)], axis=0)
    weighted = (link_all[None, :, :] * dirs[:, None, :]).reshape(2 * 2 * blk, 2 * blk)
    middle = jnp.dot(weighted, link_own, precision=lax.Precision.HIGHEST).reshape(2, 2 * blk, blk)
    closed = middle * link_own[None]
    ends = jnp.einsum('ai,bik->abk', dirs, closed, precision=lax.Precision.HIGHEST)
    last = dirs[:, blk:]
    triple_terms = (ends[:, :, None, :] * last[None, None, :, :]).reshape(8, blk)
    triples = jnp.dot(triple_terms, owners_hot, precision=lax.Precision.HIGHEST)
    return pairs, triples


def reference(stamps, account, kind, weight, used):
    shape5 = (N_GRP, N_DEV, N_DEV, NB, CAP)
    live = used.reshape(N_GRP, N_DEV, N_DEV, NB)[..., None] > jnp.arange(CAP).astype(jnp.int32)
    wt = jnp.where(live, weight.reshape(shape5).astype(jnp.float32), jnp.float32(0.0))
    fields = [stamps.reshape(shape5).astype(jnp.float32),
              account.reshape(shape5).astype(jnp.float32),
              kind.reshape(shape5).astype(jnp.float32), wt]
    arranged = [f.transpose(0, 2, 3, 1, 4).reshape(N_GRP, N_DEV, NB, BLK) for f in fields]
    stacked = jnp.stack(arranged, axis=3)
    prior = jnp.concatenate([jnp.zeros_like(stacked[:1]), stacked[:-1]], axis=0)
    total = N_GRP * N_DEV * NB
    batch = 1
    for cand in (16, 8, 4, 2):
        if total % cand == 0:
            batch = cand
            break
    own_b = stacked.reshape(total // batch, batch, 4, BLK)
    prior_b = prior.reshape(total // batch, batch, 4, BLK)
    pairs, triples = lax.map(lambda xs: jax.vmap(count_block)(xs[0], xs[1]), (own_b, prior_b))
    pairs = pairs.reshape(N_GRP, N_DEV, NB, 36, ACC_BLK).sum(axis=0)
    triples = triples.reshape(N_GRP, N_DEV, NB, 8, ACC_BLK).sum(axis=0)
    pair_profile = pairs.transpose(2, 0, 1, 3).reshape(36, ACCOUNTS)
    triple_profile = triples.transpose(2, 0, 1, 3).reshape(8, ACCOUNTS)
    return (pair_profile, triple_profile)
```

```python
import math

import jax
import jax.numpy as jnp
from jax import lax
from jax.sharding import PartitionSpec as P

DELTA = 3600
ACC_BLK = 16


def passed_along(block, axis, distance):
    devices = range(lax.axis_size(axis))
    route = [(i - distance, i) for i in devices if i - distance in devices]
    return lax.ppermute(block, axis, route)


def summed_over(block, axis):
    n = lax.axis_size(axis)
    if n & (n - 1) == 0:
        step = 1
        while step < n:
            block = block + lax.ppermute(block, axis, [(i, i ^ step) for i in range(n)])
            step *= 2
        return block
    parts = [block]
    moving = block
    for d in range(1, n):
        moving = lax.ppermute(moving, axis, [(i, (i + 1) % n) for i in range(n)])
        parts.append(moving)
    idx = lax.axis_index(axis)
    ordered = jnp.stack(parts)[(idx - jnp.arange(n)) % n]
    return ordered.sum(axis=0)


def count_block(own_rows, prior_rows):
    fields = jnp.concatenate([prior_rows, own_rows], axis=1)
    stamp, local, kinds, wt = (fields[0], fields[1], fields[2], fields[3])
    blk = own_rows.shape[1]
    gap = stamp[None, :] - stamp[:, None]
    linked = (local[:, None] == local[None, :]) & (gap > 0.0) & (gap <= DELTA)
    link_all = linked.astype(jnp.bfloat16)
    link_own = link_all[:, blk:]
    classes = (kinds[:, None] == jnp.arange(6).astype(jnp.float32)[None, :]).astype(
        jnp.float32
    ) * wt[:, None]
    earlier = jnp.einsum(
        "ik,ic->kc", link_own, classes.astype(jnp.bfloat16), preferred_element_type=jnp.float32
    )
    later = classes[blk:]
    pair_terms = (earlier[:, :, None] * later[:, None, :]).reshape(blk, 36)
    owners_hot = (local[blk:, None] == jnp.arange(ACC_BLK).astype(jnp.float32)[None, :]).astype(
        jnp.float32
    )
    pairs = jnp.dot(pair_terms.T, owners_hot, precision=lax.Precision.HIGHEST)
    dirs = jnp.stack([wt * (kinds < 2.5), wt * (kinds > 2.5)], axis=0)
    weighted = (link_all[None, :, :] * dirs.astype(jnp.bfloat16)[:, None, :]).reshape(
        2 * 2 * blk, 2 * blk
    )
    middle = jnp.dot(weighted, link_own, preferred_element_type=jnp.float32).reshape(
        2, 2 * blk, blk
    )
    closed = middle * link_own.astype(jnp.float32)[None]
    ends = jnp.einsum("ai,bik->abk", dirs, closed, precision=lax.Precision.HIGHEST)
    last = dirs[:, blk:]
    triple_terms = (ends[:, :, None, :] * last[None, None, :, :]).reshape(8, blk)
    triples = jnp.dot(triple_terms, owners_hot, precision=lax.Precision.HIGHEST)
    return (pairs, triples)


def per_device(stamps, account, kind, weight, used):
    owners = lax.axis_size("dev")
    blocks = used.shape[1] // owners
    slots = stamps.shape[0] // (owners * blocks)
    shape3 = (owners, blocks, slots)
    live = used.reshape(owners, blocks, 1) > jnp.arange(slots)
    wt = jnp.where(live, weight.reshape(shape3).astype(jnp.float32), jnp.float32(0.0))
    stacked = jnp.stack(
        [
            stamps.reshape(shape3).astype(jnp.float32),
            account.reshape(shape3).astype(jnp.float32),
            kind.reshape(shape3).astype(jnp.float32),
            wt,
        ],
        axis=2,
    )
    own_events = lax.all_to_all(stacked, "dev", split_axis=0, concat_axis=3, tiled=True)[0]
    prior_events = passed_along(own_events, "grp", 1)
    width = own_events.shape[2]
    batch = math.gcd(blocks, 16)
    own_b = own_events.reshape(blocks // batch, batch, 4, width)
    prior_b = prior_events.reshape(blocks // batch, batch, 4, width)
    pairs, triples = lax.map(lambda xs: jax.vmap(count_block)(xs[0], xs[1]), (own_b, prior_b))
    pairs = pairs.reshape(blocks, 36, ACC_BLK).transpose(1, 0, 2).reshape(36, blocks * ACC_BLK)
    triples = triples.reshape(blocks, 8, ACC_BLK).transpose(1, 0, 2).reshape(8, blocks * ACC_BLK)
    both = summed_over(jnp.concatenate([pairs, triples], axis=0), "grp")
    return (both[:36], both[36:])


def solution(mesh):
    return jax.shard_map(
        per_device,
        mesh=mesh,
        in_specs=(
            P(("grp", "dev")),
            P(("grp", "dev")),
            P(("grp", "dev")),
            P(("grp", "dev")),
            P(("grp", "dev"), None),
        ),
        out_specs=(P(None, "dev"), P(None, "dev")),
        check_vma=False,
    )
```

```python
import math

import jax
import jax.numpy as jnp
from jax import lax
from jax.experimental import pallas as pl
from jax.sharding import PartitionSpec as P

DELTA = 3600
ACC_BLK = 16


def passed_along(block, axis, distance):
    devices = range(lax.axis_size(axis))
    route = [(i - distance, i) for i in devices if i - distance in devices]
    return lax.ppermute(block, axis, route)


def summed_over(block, axis):
    n = lax.axis_size(axis)
    if n & (n - 1) == 0:
        step = 1
        while step < n:
            block = block + lax.ppermute(block, axis, [(i, i ^ step) for i in range(n)])
            step *= 2
        return block
    parts = [block]
    moving = block
    for d in range(1, n):
        moving = lax.ppermute(moving, axis, [(i, (i + 1) % n) for i in range(n)])
        parts.append(moving)
    idx = lax.axis_index(axis)
    ordered = jnp.stack(parts)[(idx - jnp.arange(n)) % n]
    return ordered.sum(axis=0)


def count_block(own_rows, prior_rows):
    fields = jnp.concatenate([prior_rows, own_rows], axis=1)
    stamp, local, kinds, wt = (fields[0], fields[1], fields[2], fields[3])
    blk = own_rows.shape[1]
    gap = stamp[None, :] - stamp[:, None]
    linked = (local[:, None] == local[None, :]) & (gap > 0.0) & (gap <= DELTA)
    link_all = linked.astype(jnp.bfloat16)
    link_own = link_all[:, blk:]
    classes = (kinds[:, None] == jnp.arange(6).astype(jnp.float32)[None, :]).astype(
        jnp.float32
    ) * wt[:, None]
    earlier = jnp.einsum(
        "ik,ic->kc", link_own, classes.astype(jnp.bfloat16), preferred_element_type=jnp.float32
    )
    later = classes[blk:]
    pair_terms = (earlier[:, :, None] * later[:, None, :]).reshape(blk, 36)
    owners_hot = (local[blk:, None] == jnp.arange(ACC_BLK).astype(jnp.float32)[None, :]).astype(
        jnp.float32
    )
    pairs = jnp.dot(pair_terms.T, owners_hot, precision=lax.Precision.HIGHEST)
    dirs = jnp.stack([wt * (kinds < 2.5), wt * (kinds > 2.5)], axis=0)
    weighted = (link_all[None, :, :] * dirs.astype(jnp.bfloat16)[:, None, :]).reshape(
        2 * 2 * blk, 2 * blk
    )
    middle = jnp.dot(weighted, link_own, preferred_element_type=jnp.float32).reshape(
        2, 2 * blk, blk
    )
    closed = middle * link_own.astype(jnp.float32)[None]
    ends = jnp.einsum("ai,bik->abk", dirs, closed, precision=lax.Precision.HIGHEST)
    last = dirs[:, blk:]
    triple_terms = (ends[:, :, None, :] * last[None, None, :, :]).reshape(8, blk)
    triples = jnp.dot(triple_terms, owners_hot, precision=lax.Precision.HIGHEST)
    return (pairs, triples)


def motif_kernel(r_ref, c_ref, pair_ref, trip_ref):
    n = r_ref.shape[-1]
    blk = n // 2
    st_r, lo_r, ki_r, wt_r = (r_ref[0:1, :], r_ref[1:2, :], r_ref[2:3, :], r_ref[3:4, :])
    st_c, lo_c = (c_ref[:, 0:1], c_ref[:, 1:2])
    gap = st_r - st_c
    link = jnp.where((lo_c == lo_r) & (gap > 0.0) & (gap <= DELTA), 1.0, 0.0)
    link_own = link[:, blk:]
    link_own16 = link_own.astype(jnp.bfloat16)
    row = lax.broadcasted_iota(jnp.int32, (8, n), 0).astype(jnp.float32)
    classes_t = jnp.where(ki_r == row, wt_r, 0.0)
    earlier_t = jnp.dot(
        classes_t.astype(jnp.bfloat16), link_own16, preferred_element_type=jnp.float32
    )
    lo_o, ki_o, wt_o = (c_ref[blk:, 1:2], c_ref[blk:, 2:3], c_ref[blk:, 3:4])
    lane = lax.broadcasted_iota(jnp.int32, (blk, 128), 1)
    lane_acc = (lane % ACC_BLK).astype(jnp.float32)
    lane_grp = (lane // ACC_BLK).astype(jnp.float32)
    later = jnp.where((lo_o == lane_acc) & (ki_o == lane_grp), wt_o, 0.0)
    pair_ref[...] = jnp.dot(
        earlier_t, later, precision=lax.Precision.HIGHEST, preferred_element_type=jnp.float32
    )
    dirs = jnp.where(
        row == 0.0, jnp.where(ki_r < 2.5, wt_r, 0.0), jnp.where(row == 1.0, jnp.where(ki_r > 2.5, wt_r, 0.0), 0.0)
    )
    wt_in = jnp.where(ki_o < 2.5, wt_o, 0.0)
    wt_out = jnp.where(ki_o > 2.5, wt_o, 0.0)
    last = jnp.where(
        lo_o == lane_acc,
        jnp.where(lane_grp == 0.0, wt_in, jnp.where(lane_grp == 1.0, wt_out, 0.0)),
        0.0,
    )
    for b in range(2):
        weighted = (link * dirs[b : b + 1, :]).astype(jnp.bfloat16)
        middle = jnp.dot(weighted, link_own16, preferred_element_type=jnp.float32)
        closed = middle * link_own
        ends = jnp.dot(dirs, closed, precision=lax.Precision.HIGHEST, preferred_element_type=jnp.float32)
        trip_ref[b] = jnp.dot(
            ends, last, precision=lax.Precision.HIGHEST, preferred_element_type=jnp.float32
        )


def count_blocks(own_events, prior_events):
    nb, nf, width = own_events.shape
    fields = jnp.concatenate([prior_events, own_events], axis=2)
    rows = jnp.concatenate([fields, jnp.zeros((nb, 8 - nf, 2 * width), fields.dtype)], axis=1)
    cols = fields.transpose(0, 2, 1)
    pair_out, trip_out = pl.pallas_call(
        motif_kernel,
        grid=(nb,),
        in_specs=[
            pl.BlockSpec((None, 8, 2 * width), lambda i: (i, 0, 0)),
            pl.BlockSpec((None, 2 * width, nf), lambda i: (i, 0, 0)),
        ],
        out_specs=[
            pl.BlockSpec((None, 8, 128), lambda i: (i, 0, 0)),
            pl.BlockSpec((None, 2, 8, 128), lambda i: (i, 0, 0, 0)),
        ],
        out_shape=[
            jax.ShapeDtypeStruct((nb, 8, 128), jnp.float32),
            jax.ShapeDtypeStruct((nb, 2, 8, 128), jnp.float32),
        ],
    )(rows, cols)
    pairs = pair_out[:, :6, : 6 * ACC_BLK].reshape(nb, 6, 6, ACC_BLK)
    pairs = pairs.transpose(1, 2, 0, 3).reshape(36, nb * ACC_BLK)
    triples = trip_out[:, :, :2, : 2 * ACC_BLK].reshape(nb, 2, 2, 2, ACC_BLK)
    triples = triples.transpose(2, 1, 3, 0, 4).reshape(8, nb * ACC_BLK)
    return (pairs, triples)


def per_device(stamps, account, kind, weight, used):
    owners = lax.axis_size("dev")
    blocks = used.shape[1] // owners
    slots = stamps.shape[0] // (owners * blocks)
    shape3 = (owners, blocks, slots)
    live = used.reshape(owners, blocks, 1) > jnp.arange(slots)
    wt = jnp.where(live, weight.reshape(shape3).astype(jnp.float32), jnp.float32(0.0))
    stacked = jnp.stack(
        [
            stamps.reshape(shape3).astype(jnp.float32),
            account.reshape(shape3).astype(jnp.float32),
            kind.reshape(shape3).astype(jnp.float32),
            wt,
        ],
        axis=2,
    )
    own_events = lax.all_to_all(stacked, "dev", split_axis=0, concat_axis=3, tiled=True)[0]
    prior_events = passed_along(own_events, "grp", 1)
    pairs, triples = count_blocks(own_events, prior_events)
    both = summed_over(jnp.concatenate([pairs, triples], axis=0), "grp")
    return (both[:36], both[36:])


def solution(mesh):
    return jax.shard_map(
        per_device,
        mesh=mesh,
        in_specs=(
            P(("grp", "dev")),
            P(("grp", "dev")),
            P(("grp", "dev")),
            P(("grp", "dev")),
            P(("grp", "dev"), None),
        ),
        out_specs=(P(None, "dev"), P(None, "dev")),
        check_vma=False,
    )
```

```python
import math

import jax
import jax.numpy as jnp
from jax import lax
from jax.experimental import pallas as pl
from jax.sharding import PartitionSpec as P

DELTA = 3600
ACC_BLK = 16


def passed_along(block, axis, distance):
    devices = range(lax.axis_size(axis))
    route = [(i - distance, i) for i in devices if i - distance in devices]
    return lax.ppermute(block, axis, route)


def summed_over(block, axis):
    n = lax.axis_size(axis)
    if n & (n - 1) == 0:
        step = 1
        while step < n:
            block = block + lax.ppermute(block, axis, [(i, i ^ step) for i in range(n)])
            step *= 2
        return block
    parts = [block]
    moving = block
    for d in range(1, n):
        moving = lax.ppermute(moving, axis, [(i, (i + 1) % n) for i in range(n)])
        parts.append(moving)
    idx = lax.axis_index(axis)
    ordered = jnp.stack(parts)[(idx - jnp.arange(n)) % n]
    return ordered.sum(axis=0)


def count_block(own_rows, prior_rows):
    fields = jnp.concatenate([prior_rows, own_rows], axis=1)
    stamp, local, kinds, wt = (fields[0], fields[1], fields[2], fields[3])
    blk = own_rows.shape[1]
    gap = stamp[None, :] - stamp[:, None]
    linked = (local[:, None] == local[None, :]) & (gap > 0.0) & (gap <= DELTA)
    link_all = linked.astype(jnp.bfloat16)
    link_own = link_all[:, blk:]
    classes = (kinds[:, None] == jnp.arange(6).astype(jnp.float32)[None, :]).astype(
        jnp.float32
    ) * wt[:, None]
    earlier = jnp.einsum(
        "ik,ic->kc", link_own, classes.astype(jnp.bfloat16), preferred_element_type=jnp.float32
    )
    later = classes[blk:]
    pair_terms = (earlier[:, :, None] * later[:, None, :]).reshape(blk, 36)
    owners_hot = (local[blk:, None] == jnp.arange(ACC_BLK).astype(jnp.float32)[None, :]).astype(
        jnp.float32
    )
    pairs = jnp.dot(pair_terms.T, owners_hot, precision=lax.Precision.HIGHEST)
    dirs = jnp.stack([wt * (kinds < 2.5), wt * (kinds > 2.5)], axis=0)
    weighted = (link_all[None, :, :] * dirs.astype(jnp.bfloat16)[:, None, :]).reshape(
        2 * 2 * blk, 2 * blk
    )
    middle = jnp.dot(weighted, link_own, preferred_element_type=jnp.float32).reshape(
        2, 2 * blk, blk
    )
    closed = middle * link_own.astype(jnp.float32)[None]
    ends = jnp.einsum("ai,bik->abk", dirs, closed, precision=lax.Precision.HIGHEST)
    last = dirs[:, blk:]
    triple_terms = (ends[:, :, None, :] * last[None, None, :, :]).reshape(8, blk)
    triples = jnp.dot(triple_terms, owners_hot, precision=lax.Precision.HIGHEST)
    return (pairs, triples)


def motif_kernel(r_ref, c_ref, pair_ref, trip_ref):
    n = r_ref.shape[-1]
    blk = n // 2
    key_r, ki_r, wt_r = (r_ref[4:5, :], r_ref[2:3, :], r_ref[3:4, :])
    gap = key_r - c_ref[:, 4:5]
    linked = (gap > 0.0) & (gap <= DELTA)
    link16 = jnp.where(linked, 1.0, 0.0).astype(jnp.bfloat16)
    linked_own = linked[:, blk:]
    link_own16 = link16[:, blk:]
    row = lax.broadcasted_iota(jnp.int32, (8, n), 0).astype(jnp.float32)
    classes_t = jnp.where(ki_r == row, wt_r, 0.0)
    earlier_t = jnp.dot(
        classes_t.astype(jnp.bfloat16), link_own16, preferred_element_type=jnp.float32
    )
    lo_o, ki_o, wt_o = (c_ref[blk:, 1:2], c_ref[blk:, 2:3], c_ref[blk:, 3:4])
    lane = lax.broadcasted_iota(jnp.int32, (blk, 128), 1)
    lane_acc = (lane % ACC_BLK).astype(jnp.float32)
    lane_grp = (lane // ACC_BLK).astype(jnp.float32)
    later = jnp.where((lo_o == lane_acc) & (ki_o == lane_grp), wt_o, 0.0)
    pair_ref[...] = jnp.dot(
        earlier_t, later, precision=lax.Precision.HIGHEST, preferred_element_type=jnp.float32
    )
    dirs = jnp.where(
        row == 0.0, jnp.where(ki_r < 2.5, wt_r, 0.0), jnp.where(row == 1.0, jnp.where(ki_r > 2.5, wt_r, 0.0), 0.0)
    )
    ki_c, wt_c = (c_ref[:, 2:3], c_ref[:, 3:4])
    d_in = jnp.where(ki_c < 2.5, wt_c, 0.0)
    d_out = jnp.where(ki_c > 2.5, wt_c, 0.0)
    scaled = jnp.concatenate(
        [jnp.where(linked_own, d_in, 0.0), jnp.where(linked_own, d_out, 0.0)], axis=1
    ).astype(jnp.bfloat16)
    middle = jnp.dot(link16, scaled, preferred_element_type=jnp.float32)
    closed = jnp.where(jnp.concatenate([linked_own, linked_own], axis=1), middle, 0.0)
    ends = jnp.dot(dirs, closed, precision=lax.Precision.HIGH, preferred_element_type=jnp.float32)
    wt_in = jnp.where(ki_o < 2.5, wt_o, 0.0)
    wt_out = jnp.where(ki_o > 2.5, wt_o, 0.0)
    last = jnp.where(
        lo_o == lane_acc,
        jnp.where(lane_grp == 0.0, wt_in, jnp.where(lane_grp == 1.0, wt_out, 0.0)),
        0.0,
    )
    for b in range(2):
        trip_ref[b] = jnp.dot(
            ends[:, b * blk : (b + 1) * blk],
            last,
            precision=lax.Precision.HIGHEST,
            preferred_element_type=jnp.float32,
        )


def count_blocks(own_events, prior_events):
    nb, nf, width = own_events.shape
    fields = jnp.concatenate([prior_events, own_events], axis=2)
    key = fields[:, 1:2] * 131072.0 + fields[:, 0:1]
    rows = jnp.concatenate([fields, key, jnp.zeros((nb, 3, 2 * width), fields.dtype)], axis=1)
    cols = rows[:, :5].transpose(0, 2, 1)
    pair_out, trip_out = pl.pallas_call(
        motif_kernel,
        grid=(nb,),
        in_specs=[
            pl.BlockSpec((None, 8, 2 * width), lambda i: (i, 0, 0)),
            pl.BlockSpec((None, 2 * width, 5), lambda i: (i, 0, 0)),
        ],
        out_specs=[
            pl.BlockSpec((None, 8, 128), lambda i: (i, 0, 0)),
            pl.BlockSpec((None, 2, 8, 128), lambda i: (i, 0, 0, 0)),
        ],
        out_shape=[
            jax.ShapeDtypeStruct((nb, 8, 128), jnp.float32),
            jax.ShapeDtypeStruct((nb, 2, 8, 128), jnp.float32),
        ],
    )(rows, cols)
    pairs = pair_out[:, :6, : 6 * ACC_BLK].reshape(nb, 6, 6, ACC_BLK)
    pairs = pairs.transpose(1, 2, 0, 3).reshape(36, nb * ACC_BLK)
    triples = trip_out[:, :, :2, : 2 * ACC_BLK].reshape(nb, 2, 2, 2, ACC_BLK)
    triples = triples.transpose(2, 1, 3, 0, 4).reshape(8, nb * ACC_BLK)
    return (pairs, triples)


def per_device(stamps, account, kind, weight, used):
    owners = lax.axis_size("dev")
    blocks = used.shape[1] // owners
    slots = stamps.shape[0] // (owners * blocks)
    shape3 = (owners, blocks, slots)
    live = used.reshape(owners, blocks, 1) > jnp.arange(slots)
    wt = jnp.where(live, weight.reshape(shape3).astype(jnp.float32), jnp.float32(0.0))
    stacked = jnp.stack(
        [
            stamps.reshape(shape3).astype(jnp.float32),
            account.reshape(shape3).astype(jnp.float32),
            kind.reshape(shape3).astype(jnp.float32),
            wt,
        ],
        axis=2,
    )
    own_events = lax.all_to_all(stacked, "dev", split_axis=0, concat_axis=3, tiled=True)[0]
    prior_events = passed_along(own_events, "grp", 1)
    pairs, triples = count_blocks(own_events, prior_events)
    both = summed_over(jnp.concatenate([pairs, triples], axis=0), "grp")
    return (both[:36], both[36:])


def solution(mesh):
    return jax.shard_map(
        per_device,
        mesh=mesh,
        in_specs=(
            P(("grp", "dev")),
            P(("grp", "dev")),
            P(("grp", "dev")),
            P(("grp", "dev")),
            P(("grp", "dev"), None),
        ),
        out_specs=(P(None, "dev"), P(None, "dev")),
        check_vma=False,
    )
```

```python
import math

import jax
import jax.numpy as jnp
from jax import lax
from jax.experimental import pallas as pl
from jax.sharding import PartitionSpec as P

DELTA = 3600
ACC_BLK = 16


def passed_along(block, axis, distance):
    devices = range(lax.axis_size(axis))
    route = [(i - distance, i) for i in devices if i - distance in devices]
    return lax.ppermute(block, axis, route)


def summed_over(block, axis):
    n = lax.axis_size(axis)
    if n <= 8:
        parts = [block] + [
            lax.ppermute(block, axis, [(i, (i + d) % n) for i in range(n)]) for d in range(1, n)
        ]
        idx = lax.axis_index(axis)
        ordered = jnp.stack(parts)[(idx - jnp.arange(n)) % n]
        total = ordered[0]
        for src in range(1, n):
            total = total + ordered[src]
        return total
    step = 1
    while step < n:
        block = block + lax.ppermute(block, axis, [(i, i ^ step) for i in range(n)])
        step *= 2
    return block


def count_block(own_rows, prior_rows):
    fields = jnp.concatenate([prior_rows, own_rows], axis=1)
    stamp, local, kinds, wt = (fields[0], fields[1], fields[2], fields[3])
    blk = own_rows.shape[1]
    gap = stamp[None, :] - stamp[:, None]
    linked = (local[:, None] == local[None, :]) & (gap > 0.0) & (gap <= DELTA)
    link_all = linked.astype(jnp.bfloat16)
    link_own = link_all[:, blk:]
    classes = (kinds[:, None] == jnp.arange(6).astype(jnp.float32)[None, :]).astype(
        jnp.float32
    ) * wt[:, None]
    earlier = jnp.einsum(
        "ik,ic->kc", link_own, classes.astype(jnp.bfloat16), preferred_element_type=jnp.float32
    )
    later = classes[blk:]
    pair_terms = (earlier[:, :, None] * later[:, None, :]).reshape(blk, 36)
    owners_hot = (local[blk:, None] == jnp.arange(ACC_BLK).astype(jnp.float32)[None, :]).astype(
        jnp.float32
    )
    pairs = jnp.dot(pair_terms.T, owners_hot, precision=lax.Precision.HIGHEST)
    dirs = jnp.stack([wt * (kinds < 2.5), wt * (kinds > 2.5)], axis=0)
    weighted = (link_all[None, :, :] * dirs.astype(jnp.bfloat16)[:, None, :]).reshape(
        2 * 2 * blk, 2 * blk
    )
    middle = jnp.dot(weighted, link_own, preferred_element_type=jnp.float32).reshape(
        2, 2 * blk, blk
    )
    closed = middle * link_own.astype(jnp.float32)[None]
    ends = jnp.einsum("ai,bik->abk", dirs, closed, precision=lax.Precision.HIGHEST)
    last = dirs[:, blk:]
    triple_terms = (ends[:, :, None, :] * last[None, None, :, :]).reshape(8, blk)
    triples = jnp.dot(triple_terms, owners_hot, precision=lax.Precision.HIGHEST)
    return (pairs, triples)


def motif_kernel(r_ref, c_ref, pair_ref, trip_ref):
    n = r_ref.shape[-1]
    blk = n // 2
    key_r, ki_r, wt_r = (r_ref[4:5, :], r_ref[2:3, :], r_ref[3:4, :])
    gap = key_r - c_ref[:, 4:5]
    linked = (gap > 0.0) & (gap <= DELTA)
    link16 = jnp.where(linked, 1.0, 0.0).astype(jnp.bfloat16)
    linked_own = linked[:, blk:]
    link_own16 = link16[:, blk:]
    row = lax.broadcasted_iota(jnp.int32, (8, n), 0).astype(jnp.float32)
    classes_t = jnp.where(ki_r == row, wt_r, 0.0)
    earlier_t = jnp.dot(
        classes_t.astype(jnp.bfloat16), link_own16, preferred_element_type=jnp.float32
    )
    lo_o, ki_o, wt_o = (c_ref[blk:, 1:2], c_ref[blk:, 2:3], c_ref[blk:, 3:4])
    lane = lax.broadcasted_iota(jnp.int32, (blk, 128), 1)
    lane_acc = (lane % ACC_BLK).astype(jnp.float32)
    lane_grp = (lane // ACC_BLK).astype(jnp.float32)
    later = jnp.where((lo_o == lane_acc) & (ki_o == lane_grp), wt_o, 0.0)
    pair_ref[...] = jnp.dot(
        earlier_t, later, precision=lax.Precision.HIGHEST, preferred_element_type=jnp.float32
    )
    dirs = jnp.where(
        row == 0.0, jnp.where(ki_r < 2.5, wt_r, 0.0), jnp.where(row == 1.0, jnp.where(ki_r > 2.5, wt_r, 0.0), 0.0)
    )
    ki_c, wt_c = (c_ref[:, 2:3], c_ref[:, 3:4])
    d_in = jnp.where(ki_c < 2.5, wt_c, 0.0)
    d_out = jnp.where(ki_c > 2.5, wt_c, 0.0)
    scaled = jnp.concatenate(
        [jnp.where(linked_own, d_in, 0.0), jnp.where(linked_own, d_out, 0.0)], axis=1
    ).astype(jnp.bfloat16)
    middle = jnp.dot(link16, scaled, preferred_element_type=jnp.float32)
    closed = jnp.where(jnp.concatenate([linked_own, linked_own], axis=1), middle, 0.0)
    ends = jnp.dot(dirs, closed, precision=lax.Precision.HIGH, preferred_element_type=jnp.float32)
    wt_in = jnp.where(ki_o < 2.5, wt_o, 0.0)
    wt_out = jnp.where(ki_o > 2.5, wt_o, 0.0)
    last = jnp.where(
        lo_o == lane_acc,
        jnp.where(lane_grp == 0.0, wt_in, jnp.where(lane_grp == 1.0, wt_out, 0.0)),
        0.0,
    )
    for b in range(2):
        trip_ref[b] = jnp.dot(
            ends[:, b * blk : (b + 1) * blk],
            last,
            precision=lax.Precision.HIGHEST,
            preferred_element_type=jnp.float32,
        )


def count_blocks(own_events, prior_events):
    nb, nf, width = own_events.shape
    fields = jnp.concatenate([prior_events, own_events], axis=2)
    key = fields[:, 1:2] * 131072.0 + fields[:, 0:1]
    rows = jnp.concatenate([fields, key, jnp.zeros((nb, 3, 2 * width), fields.dtype)], axis=1)
    cols = rows[:, :5].transpose(0, 2, 1)
    pair_out, trip_out = pl.pallas_call(
        motif_kernel,
        grid=(nb,),
        in_specs=[
            pl.BlockSpec((None, 8, 2 * width), lambda i: (i, 0, 0)),
            pl.BlockSpec((None, 2 * width, 5), lambda i: (i, 0, 0)),
        ],
        out_specs=[
            pl.BlockSpec((None, 8, 128), lambda i: (i, 0, 0)),
            pl.BlockSpec((None, 2, 8, 128), lambda i: (i, 0, 0, 0)),
        ],
        out_shape=[
            jax.ShapeDtypeStruct((nb, 8, 128), jnp.float32),
            jax.ShapeDtypeStruct((nb, 2, 8, 128), jnp.float32),
        ],
    )(rows, cols)
    pairs = pair_out[:, :6, : 6 * ACC_BLK].reshape(nb, 6, 6, ACC_BLK)
    pairs = pairs.transpose(1, 2, 0, 3).reshape(36, nb * ACC_BLK)
    triples = trip_out[:, :, :2, : 2 * ACC_BLK].reshape(nb, 2, 2, 2, ACC_BLK)
    triples = triples.transpose(2, 1, 3, 0, 4).reshape(8, nb * ACC_BLK)
    return (pairs, triples)


def per_device(stamps, account, kind, weight, used):
    owners = lax.axis_size("dev")
    blocks = used.shape[1] // owners
    slots = stamps.shape[0] // (owners * blocks)
    shape3 = (owners, blocks, slots)
    live = used.reshape(owners, blocks, 1) > jnp.arange(slots)
    wt = jnp.where(live, weight.reshape(shape3).astype(jnp.float32), jnp.float32(0.0))
    stacked = jnp.stack(
        [
            stamps.reshape(shape3).astype(jnp.float32),
            account.reshape(shape3).astype(jnp.float32),
            kind.reshape(shape3).astype(jnp.float32),
            wt,
        ],
        axis=2,
    )
    own_events = lax.all_to_all(stacked, "dev", split_axis=0, concat_axis=3, tiled=True)[0]
    prior_events = passed_along(own_events, "grp", 1)
    pairs, triples = count_blocks(own_events, prior_events)
    both = summed_over(jnp.concatenate([pairs, triples], axis=0), "grp")
    return (both[:36], both[36:])


def solution(mesh):
    return jax.shard_map(
        per_device,
        mesh=mesh,
        in_specs=(
            P(("grp", "dev")),
            P(("grp", "dev")),
            P(("grp", "dev")),
            P(("grp", "dev")),
            P(("grp", "dev"), None),
        ),
        out_specs=(P(None, "dev"), P(None, "dev")),
        check_vma=False,
    )
```

```python
import math

import jax
import jax.numpy as jnp
from jax import lax
from jax.experimental import pallas as pl
from jax.sharding import PartitionSpec as P

DELTA = 3600
ACC_BLK = 16


def passed_along(block, axis, distance):
    devices = range(lax.axis_size(axis))
    route = [(i - distance, i) for i in devices if i - distance in devices]
    return lax.ppermute(block, axis, route)


def summed_over(block, axis):
    n = lax.axis_size(axis)
    if n & (n - 1) == 0:
        step = 1
        while step < n:
            block = block + lax.ppermute(block, axis, [(i, i ^ step) for i in range(n)])
            step *= 2
        return block
    parts = [block]
    moving = block
    for d in range(1, n):
        moving = lax.ppermute(moving, axis, [(i, (i + 1) % n) for i in range(n)])
        parts.append(moving)
    idx = lax.axis_index(axis)
    ordered = jnp.stack(parts)[(idx - jnp.arange(n)) % n]
    return ordered.sum(axis=0)


def count_block(own_rows, prior_rows):
    fields = jnp.concatenate([prior_rows, own_rows], axis=1)
    stamp, local, kinds, wt = (fields[0], fields[1], fields[2], fields[3])
    blk = own_rows.shape[1]
    gap = stamp[None, :] - stamp[:, None]
    linked = (local[:, None] == local[None, :]) & (gap > 0.0) & (gap <= DELTA)
    link_all = linked.astype(jnp.bfloat16)
    link_own = link_all[:, blk:]
    classes = (kinds[:, None] == jnp.arange(6).astype(jnp.float32)[None, :]).astype(
        jnp.float32
    ) * wt[:, None]
    earlier = jnp.einsum(
        "ik,ic->kc", link_own, classes.astype(jnp.bfloat16), preferred_element_type=jnp.float32
    )
    later = classes[blk:]
    pair_terms = (earlier[:, :, None] * later[:, None, :]).reshape(blk, 36)
    owners_hot = (local[blk:, None] == jnp.arange(ACC_BLK).astype(jnp.float32)[None, :]).astype(
        jnp.float32
    )
    pairs = jnp.dot(pair_terms.T, owners_hot, precision=lax.Precision.HIGHEST)
    dirs = jnp.stack([wt * (kinds < 2.5), wt * (kinds > 2.5)], axis=0)
    weighted = (link_all[None, :, :] * dirs.astype(jnp.bfloat16)[:, None, :]).reshape(
        2 * 2 * blk, 2 * blk
    )
    middle = jnp.dot(weighted, link_own, preferred_element_type=jnp.float32).reshape(
        2, 2 * blk, blk
    )
    closed = middle * link_own.astype(jnp.float32)[None]
    ends = jnp.einsum("ai,bik->abk", dirs, closed, precision=lax.Precision.HIGHEST)
    last = dirs[:, blk:]
    triple_terms = (ends[:, :, None, :] * last[None, None, :, :]).reshape(8, blk)
    triples = jnp.dot(triple_terms, owners_hot, precision=lax.Precision.HIGHEST)
    return (pairs, triples)


def motif_kernel(r_ref, pair_ref, trip_ref):
    c_ref = jnp.transpose(r_ref[...])
    n = r_ref.shape[-1]
    blk = n // 2
    key_r, ki_r, wt_r = (r_ref[4:5, :], r_ref[2:3, :], r_ref[3:4, :])
    gap = key_r - c_ref[:, 4:5]
    linked = (gap > 0.0) & (gap <= DELTA)
    link16 = jnp.where(linked, 1.0, 0.0).astype(jnp.bfloat16)
    linked_own = linked[:, blk:]
    link_own16 = link16[:, blk:]
    row = lax.broadcasted_iota(jnp.int32, (8, n), 0).astype(jnp.float32)
    classes_t = jnp.where(ki_r == row, wt_r, 0.0)
    earlier_t = jnp.dot(
        classes_t.astype(jnp.bfloat16), link_own16, preferred_element_type=jnp.float32
    )
    lo_o, ki_o, wt_o = (c_ref[blk:, 1:2], c_ref[blk:, 2:3], c_ref[blk:, 3:4])
    lane = lax.broadcasted_iota(jnp.int32, (blk, 128), 1)
    lane_acc = (lane % ACC_BLK).astype(jnp.float32)
    lane_grp = (lane // ACC_BLK).astype(jnp.float32)
    later = jnp.where((lo_o == lane_acc) & (ki_o == lane_grp), wt_o, 0.0)
    pair_ref[...] = jnp.dot(
        earlier_t, later, precision=lax.Precision.HIGHEST, preferred_element_type=jnp.float32
    )
    dirs = jnp.where(
        row == 0.0, jnp.where(ki_r < 2.5, wt_r, 0.0), jnp.where(row == 1.0, jnp.where(ki_r > 2.5, wt_r, 0.0), 0.0)
    )
    ki_c, wt_c = (c_ref[:, 2:3], c_ref[:, 3:4])
    d_in = jnp.where(ki_c < 2.5, wt_c, 0.0)
    d_out = jnp.where(ki_c > 2.5, wt_c, 0.0)
    scaled = jnp.concatenate(
        [jnp.where(linked_own, d_in, 0.0), jnp.where(linked_own, d_out, 0.0)], axis=1
    ).astype(jnp.bfloat16)
    middle = jnp.dot(link16, scaled, preferred_element_type=jnp.float32)
    closed = jnp.where(jnp.concatenate([linked_own, linked_own], axis=1), middle, 0.0)
    ends = jnp.dot(dirs, closed, precision=lax.Precision.HIGH, preferred_element_type=jnp.float32)
    wt_in = jnp.where(ki_o < 2.5, wt_o, 0.0)
    wt_out = jnp.where(ki_o > 2.5, wt_o, 0.0)
    last = jnp.where(
        lo_o == lane_acc,
        jnp.where(lane_grp == 0.0, wt_in, jnp.where(lane_grp == 1.0, wt_out, 0.0)),
        0.0,
    )
    for b in range(2):
        trip_ref[b] = jnp.dot(
            ends[:, b * blk : (b + 1) * blk],
            last,
            precision=lax.Precision.HIGHEST,
            preferred_element_type=jnp.float32,
        )


def count_blocks(own_events, prior_events):
    nb, nf, width = own_events.shape
    fields = jnp.concatenate([prior_events, own_events], axis=2)
    key = fields[:, 1:2] * 131072.0 + fields[:, 0:1]
    rows = jnp.concatenate([fields, key, jnp.zeros((nb, 3, 2 * width), fields.dtype)], axis=1)
    pair_out, trip_out = pl.pallas_call(
        motif_kernel,
        grid=(nb,),
        in_specs=[
            pl.BlockSpec((None, 8, 2 * width), lambda i: (i, 0, 0)),
        ],
        out_specs=[
            pl.BlockSpec((None, 8, 128), lambda i: (i, 0, 0)),
            pl.BlockSpec((None, 2, 8, 128), lambda i: (i, 0, 0, 0)),
        ],
        out_shape=[
            jax.ShapeDtypeStruct((nb, 8, 128), jnp.float32),
            jax.ShapeDtypeStruct((nb, 2, 8, 128), jnp.float32),
        ],
    )(rows)
    pairs = pair_out[:, :6, : 6 * ACC_BLK].reshape(nb, 6, 6, ACC_BLK)
    pairs = pairs.transpose(1, 2, 0, 3).reshape(36, nb * ACC_BLK)
    triples = trip_out[:, :, :2, : 2 * ACC_BLK].reshape(nb, 2, 2, 2, ACC_BLK)
    triples = triples.transpose(2, 1, 3, 0, 4).reshape(8, nb * ACC_BLK)
    return (pairs, triples)


def per_device(stamps, account, kind, weight, used):
    owners = lax.axis_size("dev")
    blocks = used.shape[1] // owners
    slots = stamps.shape[0] // (owners * blocks)
    shape3 = (owners, blocks, slots)
    live = used.reshape(owners, blocks, 1) > jnp.arange(slots)
    wt = jnp.where(live, weight.reshape(shape3).astype(jnp.float32), jnp.float32(0.0))
    stacked = jnp.stack(
        [
            stamps.reshape(shape3).astype(jnp.float32),
            account.reshape(shape3).astype(jnp.float32),
            kind.reshape(shape3).astype(jnp.float32),
            wt,
        ],
        axis=2,
    )
    own_events = lax.all_to_all(stacked, "dev", split_axis=0, concat_axis=3, tiled=True)[0]
    prior_events = passed_along(own_events, "grp", 1)
    pairs, triples = count_blocks(own_events, prior_events)
    both = summed_over(jnp.concatenate([pairs, triples], axis=0), "grp")
    return (both[:36], both[36:])


def solution(mesh):
    return jax.shard_map(
        per_device,
        mesh=mesh,
        in_specs=(
            P(("grp", "dev")),
            P(("grp", "dev")),
            P(("grp", "dev")),
            P(("grp", "dev")),
            P(("grp", "dev"), None),
        ),
        out_specs=(P(None, "dev"), P(None, "dev")),
        check_vma=False,
    )
```

```python
import math

import jax
import jax.numpy as jnp
from jax import lax
from jax.experimental import pallas as pl
from jax.sharding import PartitionSpec as P

DELTA = 3600
ACC_BLK = 16


def passed_along(block, axis, distance):
    devices = range(lax.axis_size(axis))
    route = [(i - distance, i) for i in devices if i - distance in devices]
    return lax.ppermute(block, axis, route)


def summed_over(block, axis):
    n = lax.axis_size(axis)
    if n & (n - 1) == 0:
        step = 1
        while step < n:
            block = block + lax.ppermute(block, axis, [(i, i ^ step) for i in range(n)])
            step *= 2
        return block
    parts = [block]
    moving = block
    for d in range(1, n):
        moving = lax.ppermute(moving, axis, [(i, (i + 1) % n) for i in range(n)])
        parts.append(moving)
    idx = lax.axis_index(axis)
    ordered = jnp.stack(parts)[(idx - jnp.arange(n)) % n]
    return ordered.sum(axis=0)


def count_block(own_rows, prior_rows):
    fields = jnp.concatenate([prior_rows, own_rows], axis=1)
    stamp, local, kinds, wt = (fields[0], fields[1], fields[2], fields[3])
    blk = own_rows.shape[1]
    gap = stamp[None, :] - stamp[:, None]
    linked = (local[:, None] == local[None, :]) & (gap > 0.0) & (gap <= DELTA)
    link_all = linked.astype(jnp.bfloat16)
    link_own = link_all[:, blk:]
    classes = (kinds[:, None] == jnp.arange(6).astype(jnp.float32)[None, :]).astype(
        jnp.float32
    ) * wt[:, None]
    earlier = jnp.einsum(
        "ik,ic->kc", link_own, classes.astype(jnp.bfloat16), preferred_element_type=jnp.float32
    )
    later = classes[blk:]
    pair_terms = (earlier[:, :, None] * later[:, None, :]).reshape(blk, 36)
    owners_hot = (local[blk:, None] == jnp.arange(ACC_BLK).astype(jnp.float32)[None, :]).astype(
        jnp.float32
    )
    pairs = jnp.dot(pair_terms.T, owners_hot, precision=lax.Precision.HIGHEST)
    dirs = jnp.stack([wt * (kinds < 2.5), wt * (kinds > 2.5)], axis=0)
    weighted = (link_all[None, :, :] * dirs.astype(jnp.bfloat16)[:, None, :]).reshape(
        2 * 2 * blk, 2 * blk
    )
    middle = jnp.dot(weighted, link_own, preferred_element_type=jnp.float32).reshape(
        2, 2 * blk, blk
    )
    closed = middle * link_own.astype(jnp.float32)[None]
    ends = jnp.einsum("ai,bik->abk", dirs, closed, precision=lax.Precision.HIGHEST)
    last = dirs[:, blk:]
    triple_terms = (ends[:, :, None, :] * last[None, None, :, :]).reshape(8, blk)
    triples = jnp.dot(triple_terms, owners_hot, precision=lax.Precision.HIGHEST)
    return (pairs, triples)


def motif_kernel(r_ref, pair_ref, trip_ref):
    c_ref = jnp.transpose(r_ref[...])
    n = r_ref.shape[-1]
    blk = n // 2
    key_r, ki_r, wt_r = (r_ref[4:5, :], r_ref[2:3, :], r_ref[3:4, :])
    gap = key_r - c_ref[:, 4:5]
    linked = (gap > 0.0) & (gap <= DELTA)
    link16 = jnp.where(linked, 1.0, 0.0).astype(jnp.bfloat16)
    linked_own = linked[:, blk:]
    link_own16 = link16[:, blk:]
    row = lax.broadcasted_iota(jnp.int32, (8, n), 0).astype(jnp.float32)
    classes_t = jnp.where(ki_r == row, wt_r, 0.0)
    earlier_t = jnp.dot(
        classes_t.astype(jnp.bfloat16), link_own16, preferred_element_type=jnp.float32
    )
    lo_o, ki_o, wt_o = (c_ref[blk:, 1:2], c_ref[blk:, 2:3], c_ref[blk:, 3:4])
    lane = lax.broadcasted_iota(jnp.int32, (blk, 128), 1)
    lane_acc = (lane % ACC_BLK).astype(jnp.float32)
    lane_grp = (lane // ACC_BLK).astype(jnp.float32)
    later = jnp.where((lo_o == lane_acc) & (ki_o == lane_grp), wt_o, 0.0)
    pair_ref[...] = jnp.dot(
        earlier_t, later, precision=lax.Precision.HIGHEST, preferred_element_type=jnp.float32
    )
    dirs = jnp.where(
        row == 0.0, jnp.where(ki_r < 2.5, wt_r, 0.0), jnp.where(row == 1.0, jnp.where(ki_r > 2.5, wt_r, 0.0), 0.0)
    )
    ki_c, wt_c = (c_ref[:, 2:3], c_ref[:, 3:4])
    d_in = jnp.where(ki_c < 2.5, wt_c, 0.0)
    d_out = jnp.where(ki_c > 2.5, wt_c, 0.0)
    scaled = jnp.concatenate(
        [jnp.where(linked_own, d_in, 0.0), jnp.where(linked_own, d_out, 0.0)], axis=1
    ).astype(jnp.bfloat16)
    middle = jnp.dot(link16, scaled, preferred_element_type=jnp.float32)
    closed = jnp.where(jnp.concatenate([linked_own, linked_own], axis=1), middle, 0.0)
    ends = jnp.dot(dirs, closed, precision=lax.Precision.HIGH, preferred_element_type=jnp.float32)
    wt_in = jnp.where(ki_o < 2.5, wt_o, 0.0)
    wt_out = jnp.where(ki_o > 2.5, wt_o, 0.0)
    last = jnp.where(
        lo_o == lane_acc,
        jnp.where(lane_grp == 0.0, wt_in, jnp.where(lane_grp == 1.0, wt_out, 0.0)),
        0.0,
    )
    for b in range(2):
        trip_ref[b] = jnp.dot(
            ends[:, b * blk : (b + 1) * blk],
            last,
            precision=lax.Precision.HIGHEST,
            preferred_element_type=jnp.float32,
        )


def count_blocks(own_events, prior_events):
    nb, nf, width = own_events.shape
    fields = jnp.concatenate([prior_events, own_events], axis=2)
    key = fields[:, 1:2] * 131072.0 + fields[:, 0:1]
    rows = jnp.concatenate([fields, key, jnp.zeros((nb, 3, 2 * width), fields.dtype)], axis=1)
    pair_out, trip_out = pl.pallas_call(
        motif_kernel,
        grid=(nb,),
        in_specs=[
            pl.BlockSpec((None, 8, 2 * width), lambda i: (i, 0, 0)),
        ],
        out_specs=[
            pl.BlockSpec((None, 8, 128), lambda i: (i, 0, 0)),
            pl.BlockSpec((None, 2, 8, 128), lambda i: (i, 0, 0, 0)),
        ],
        out_shape=[
            jax.ShapeDtypeStruct((nb, 8, 128), jnp.float32),
            jax.ShapeDtypeStruct((nb, 2, 8, 128), jnp.float32),
        ],
    )(rows)
    pairs = pair_out[:, :6, : 6 * ACC_BLK].reshape(nb, 6, 6, ACC_BLK)
    pairs = pairs.transpose(1, 2, 0, 3).reshape(36, nb * ACC_BLK)
    triples = trip_out[:, :, :2, : 2 * ACC_BLK].reshape(nb, 2, 2, 2, ACC_BLK)
    triples = triples.transpose(2, 1, 3, 0, 4).reshape(8, nb * ACC_BLK)
    return (pairs, triples)


def per_device(stamps, account, kind, weight, used):
    owners = lax.axis_size("dev")
    blocks = used.shape[1] // owners
    slots = stamps.shape[0] // (owners * blocks)
    shape3 = (owners, blocks, slots)
    live = used.reshape(owners, blocks, 1) > jnp.arange(slots)
    wt = jnp.where(live, weight.reshape(shape3).astype(jnp.float32), jnp.float32(0.0))
    stacked = jnp.stack(
        [
            stamps.reshape(shape3).astype(jnp.float32),
            account.reshape(shape3).astype(jnp.float32),
            kind.reshape(shape3).astype(jnp.float32),
            wt,
        ],
        axis=2,
    )
    own_events = lax.all_to_all(stacked, "dev", split_axis=0, concat_axis=3, tiled=True)[0]
    prior_events = passed_along(own_events, "grp", 1)
    pairs, triples = count_blocks(own_events, prior_events)
    gap_rows = jnp.zeros((4, pairs.shape[1]), pairs.dtype)
    both = summed_over(jnp.concatenate([pairs, gap_rows, triples], axis=0), "grp")
    return (both[:36], both[40:])


def solution(mesh):
    return jax.shard_map(
        per_device,
        mesh=mesh,
        in_specs=(
            P(("grp", "dev")),
            P(("grp", "dev")),
            P(("grp", "dev")),
            P(("grp", "dev")),
            P(("grp", "dev"), None),
        ),
        out_specs=(P(None, "dev"), P(None, "dev")),
        check_vma=False,
    )
```

```python
import math

import jax
import jax.numpy as jnp
from jax import lax
from jax.experimental import pallas as pl
from jax.sharding import PartitionSpec as P

DELTA = 3600
ACC_BLK = 16


def passed_along(block, axis, distance):
    devices = range(lax.axis_size(axis))
    route = [(i - distance, i) for i in devices if i - distance in devices]
    return lax.ppermute(block, axis, route)


def summed_over(block, axis):
    n = lax.axis_size(axis)
    if n & (n - 1) == 0:
        step = 1
        while step < n:
            block = block + lax.ppermute(block, axis, [(i, i ^ step) for i in range(n)])
            step *= 2
        return block
    parts = [block]
    moving = block
    for d in range(1, n):
        moving = lax.ppermute(moving, axis, [(i, (i + 1) % n) for i in range(n)])
        parts.append(moving)
    idx = lax.axis_index(axis)
    ordered = jnp.stack(parts)[(idx - jnp.arange(n)) % n]
    return ordered.sum(axis=0)


def count_block(own_rows, prior_rows):
    fields = jnp.concatenate([prior_rows, own_rows], axis=1)
    stamp, local, kinds, wt = (fields[0], fields[1], fields[2], fields[3])
    blk = own_rows.shape[1]
    gap = stamp[None, :] - stamp[:, None]
    linked = (local[:, None] == local[None, :]) & (gap > 0.0) & (gap <= DELTA)
    link_all = linked.astype(jnp.bfloat16)
    link_own = link_all[:, blk:]
    classes = (kinds[:, None] == jnp.arange(6).astype(jnp.float32)[None, :]).astype(
        jnp.float32
    ) * wt[:, None]
    earlier = jnp.einsum(
        "ik,ic->kc", link_own, classes.astype(jnp.bfloat16), preferred_element_type=jnp.float32
    )
    later = classes[blk:]
    pair_terms = (earlier[:, :, None] * later[:, None, :]).reshape(blk, 36)
    owners_hot = (local[blk:, None] == jnp.arange(ACC_BLK).astype(jnp.float32)[None, :]).astype(
        jnp.float32
    )
    pairs = jnp.dot(pair_terms.T, owners_hot, precision=lax.Precision.HIGHEST)
    dirs = jnp.stack([wt * (kinds < 2.5), wt * (kinds > 2.5)], axis=0)
    weighted = (link_all[None, :, :] * dirs.astype(jnp.bfloat16)[:, None, :]).reshape(
        2 * 2 * blk, 2 * blk
    )
    middle = jnp.dot(weighted, link_own, preferred_element_type=jnp.float32).reshape(
        2, 2 * blk, blk
    )
    closed = middle * link_own.astype(jnp.float32)[None]
    ends = jnp.einsum("ai,bik->abk", dirs, closed, precision=lax.Precision.HIGHEST)
    last = dirs[:, blk:]
    triple_terms = (ends[:, :, None, :] * last[None, None, :, :]).reshape(8, blk)
    triples = jnp.dot(triple_terms, owners_hot, precision=lax.Precision.HIGHEST)
    return (pairs, triples)


def motif_kernel(r_ref, pair_ref, trip_ref):
    c_ref = jnp.transpose(r_ref[...])
    n = r_ref.shape[-1]
    blk = n // 2
    key_r, ki_r, wt_r = (r_ref[4:5, :], r_ref[2:3, :], r_ref[3:4, :])
    gap = key_r - c_ref[:, 4:5]
    linked = (gap > 0.0) & (gap <= DELTA)
    link16 = jnp.where(linked, 1.0, 0.0).astype(jnp.bfloat16)
    linked_own = linked[:, blk:]
    link_own16 = link16[:, blk:]
    row = lax.broadcasted_iota(jnp.int32, (8, n), 0).astype(jnp.float32)
    classes_t = jnp.where(ki_r == row, wt_r, 0.0)
    earlier_t = jnp.dot(
        classes_t.astype(jnp.bfloat16), link_own16, preferred_element_type=jnp.float32
    )
    lo_o, ki_o, wt_o = (c_ref[blk:, 1:2], c_ref[blk:, 2:3], c_ref[blk:, 3:4])
    lane = lax.broadcasted_iota(jnp.int32, (blk, 128), 1)
    lane_acc = (lane % ACC_BLK).astype(jnp.float32)
    lane_grp = (lane // ACC_BLK).astype(jnp.float32)
    later = jnp.where((lo_o == lane_acc) & (ki_o == lane_grp), wt_o, 0.0)
    pair_ref[...] = jnp.dot(
        earlier_t, later, precision=lax.Precision.HIGH, preferred_element_type=jnp.float32
    )
    dirs = jnp.where(
        row == 0.0, jnp.where(ki_r < 2.5, wt_r, 0.0), jnp.where(row == 1.0, jnp.where(ki_r > 2.5, wt_r, 0.0), 0.0)
    )
    ki_c, wt_c = (c_ref[:, 2:3], c_ref[:, 3:4])
    d_in = jnp.where(ki_c < 2.5, wt_c, 0.0)
    d_out = jnp.where(ki_c > 2.5, wt_c, 0.0)
    scaled = jnp.concatenate(
        [jnp.where(linked_own, d_in, 0.0), jnp.where(linked_own, d_out, 0.0)], axis=1
    ).astype(jnp.bfloat16)
    middle = jnp.dot(link16, scaled, preferred_element_type=jnp.float32)
    closed = jnp.where(jnp.concatenate([linked_own, linked_own], axis=1), middle, 0.0)
    ends = jnp.dot(dirs, closed, precision=lax.Precision.HIGH, preferred_element_type=jnp.float32)
    wt_in = jnp.where(ki_o < 2.5, wt_o, 0.0)
    wt_out = jnp.where(ki_o > 2.5, wt_o, 0.0)
    last = jnp.where(
        lo_o == lane_acc,
        jnp.where(lane_grp == 0.0, wt_in, jnp.where(lane_grp == 1.0, wt_out, 0.0)),
        0.0,
    )
    for b in range(2):
        trip_ref[b] = jnp.dot(
            ends[:, b * blk : (b + 1) * blk],
            last,
            precision=lax.Precision.HIGH,
            preferred_element_type=jnp.float32,
        )


def count_blocks(own_events, prior_events):
    nb, nf, width = own_events.shape
    fields = jnp.concatenate([prior_events, own_events], axis=2)
    key = fields[:, 1:2] * 131072.0 + fields[:, 0:1]
    rows = jnp.concatenate([fields, key, jnp.zeros((nb, 3, 2 * width), fields.dtype)], axis=1)
    pair_out, trip_out = pl.pallas_call(
        motif_kernel,
        grid=(nb,),
        in_specs=[
            pl.BlockSpec((None, 8, 2 * width), lambda i: (i, 0, 0)),
        ],
        out_specs=[
            pl.BlockSpec((None, 8, 128), lambda i: (i, 0, 0)),
            pl.BlockSpec((None, 2, 8, 128), lambda i: (i, 0, 0, 0)),
        ],
        out_shape=[
            jax.ShapeDtypeStruct((nb, 8, 128), jnp.float32),
            jax.ShapeDtypeStruct((nb, 2, 8, 128), jnp.float32),
        ],
    )(rows)
    pairs = pair_out[:, :6, : 6 * ACC_BLK].reshape(nb, 6, 6, ACC_BLK)
    pairs = pairs.transpose(1, 2, 0, 3).reshape(36, nb * ACC_BLK)
    triples = trip_out[:, :, :2, : 2 * ACC_BLK].reshape(nb, 2, 2, 2, ACC_BLK)
    triples = triples.transpose(2, 1, 3, 0, 4).reshape(8, nb * ACC_BLK)
    return (pairs, triples)


def per_device(stamps, account, kind, weight, used):
    owners = lax.axis_size("dev")
    blocks = used.shape[1] // owners
    slots = stamps.shape[0] // (owners * blocks)
    shape3 = (owners, blocks, slots)
    live = used.reshape(owners, blocks, 1) > jnp.arange(slots)
    wt = jnp.where(live, weight.reshape(shape3).astype(jnp.float32), jnp.float32(0.0))
    stacked = jnp.stack(
        [
            stamps.reshape(shape3).astype(jnp.float32),
            account.reshape(shape3).astype(jnp.float32),
            kind.reshape(shape3).astype(jnp.float32),
            wt,
        ],
        axis=2,
    )
    own_events = lax.all_to_all(stacked, "dev", split_axis=0, concat_axis=3, tiled=True)[0]
    prior_events = passed_along(own_events, "grp", 1)
    pairs, triples = count_blocks(own_events, prior_events)
    gap_rows = jnp.zeros((4, pairs.shape[1]), pairs.dtype)
    both = summed_over(jnp.concatenate([pairs, gap_rows, triples], axis=0), "grp")
    return (both[:36], both[40:])


def solution(mesh):
    return jax.shard_map(
        per_device,
        mesh=mesh,
        in_specs=(
            P(("grp", "dev")),
            P(("grp", "dev")),
            P(("grp", "dev")),
            P(("grp", "dev")),
            P(("grp", "dev"), None),
        ),
        out_specs=(P(None, "dev"), P(None, "dev")),
        check_vma=False,
    )
```
